256 devices in a mesh: row: 4 (over y_lo, core), col: 64 (over y_hi, z, x).
Axes of the slice: x: 4, y: 4 (y_hi: 2, y_lo: 2; y = y_hi * 2 + y_lo), z: 8, core: 2. Of those that a mesh axis runs over, the one named last changes fastest.
Arguments:
- gamma: float32 [1024, 131072], P('row', 'col'), may hold values from -0.75 to 0.75
- row_gates_a: bfloat16 [4, 256, 256], P('row'), may hold values from -1 to 1, as said below
- first_column_gates: bfloat16 [256, 512, 512], P('col'), may hold values from -1 to 1, as said below
- row_gates_b: bfloat16 [4, 256, 256], P('row'), may hold values from -1 to 1, as said below
- col_gates_b: bfloat16 [256, 512, 512], P('col'), may hold values from -1 to 1, as said below
- modes: int32 [128], replicated, may hold values from 0 to 1023, as said below
- outcomes: int32 [64], replicated, may hold values from 0 to 1
Outputs:
- updated: float32 [1024, 131072], P('row', 'col')
The draws below stay inside these ranges and needn't reach their ends.
Inputs may be any that keep to these rules, and one draw needn't show every extreme that they name: `row_gates_a`: each brick is a random orthogonal matrix rounded to bfloat16. `first_column_gates`: each brick is a random orthogonal matrix rounded to bfloat16. `row_gates_b`: each brick is a random orthogonal matrix rounded to bfloat16. `col_gates_b`: each brick is a random orthogonal matrix rounded to bfloat16. `modes`: entry k lies in [k * 8, (k + 1) * 8), so the entries rise and are distinct.
All inputs are finite; a program needn't handle non-finite values.
Results may differ from the reference program's by a relative error of at most 0.0018.
Values may be sent and summed in bfloat16 or wider, within the bound.
A program may use at most 64 MiB of HBM per device.

```python
import jax
import jax.numpy as jnp
from jax import lax

RB = 256
CB = 512
MEASURED_MODES = 128
SLAB_ROWS = 1024
NMAJ = 131072


def orthogonal_bricks(key, count, width):
    raw = jax.random.normal(key, (count, width, width), jnp.float32)
    basis = jnp.linalg.qr(raw)[0]
    return basis.astype(jnp.bfloat16)


def draw_row_gates_a(key, part):
    return orthogonal_bricks(jax.random.fold_in(key, 11), SLAB_ROWS // RB, RB)


def draw_first_column_gates(key, part):
    return orthogonal_bricks(jax.random.fold_in(key, 12), NMAJ // CB, CB)


def draw_row_gates_b(key, part):
    return orthogonal_bricks(jax.random.fold_in(key, 13), SLAB_ROWS // RB, RB)


def draw_col_gates_b(key, part):
    return orthogonal_bricks(jax.random.fold_in(key, 14), NMAJ // CB, CB)


def draw_modes(key, part):
    step_spacing = SLAB_ROWS // MEASURED_MODES
    inside_block = jax.random.randint(jax.random.fold_in(key, 15), (MEASURED_MODES,), 0, step_spacing)
    return (jnp.arange(MEASURED_MODES, dtype=jnp.int32) * step_spacing + inside_block).astype(jnp.int32)


def touch_ends(drawn, key, smallest, high):
    longest = drawn.shape.index(max(drawn.shape))
    spots = []
    for shift in (0, 1):
        where = [jax.random.randint(jax.random.fold_in(key, axis), (), 0, length) for axis, length in enumerate(drawn.shape)]
        where[longest] = (where[longest] + shift) % drawn.shape[longest]
        spots.append(tuple(where))
    return drawn.at[spots[0]].set(smallest).at[spots[1]].set(high)


def steps_of(key, dims, pieces, low, top_value):
    factor_of, own = 1.0, jax.random.fold_in(key, 6)
    for axis_at, parts in pieces:
        heights = jnp.exp(jax.random.uniform(jax.random.fold_in(own, axis_at), (parts,), jnp.float32, low / len(pieces), top_value / len(pieces)))
        factor_of = factor_of * jnp.repeat(heights, dims[axis_at] // parts).reshape([-1 if axis == axis_at else 1 for axis in range(len(dims))])
    return factor_of


def scatter_about(own_key, shape, spread, limit, cuts=(), held_as=jnp.bfloat16):
    entries = jax.random.normal(own_key, shape, jnp.float32) * spread
    if len(cuts) > 0:
        entries = steps_of(own_key, shape, cuts, -0.22, 0.18) * entries
    return jnp.clip(entries, min=-limit, max=limit).astype(held_as)


def setup_inputs(seed: int = 0) -> dict:
    key_list = jax.random.split(jax.random.key(seed), 8)
    return {
        "gamma": scatter_about(key_list[0], (SLAB_ROWS, NMAJ), 0.05, 0.75, ((0, 4), (1, 64)), jnp.float32),
        "row_gates_a": draw_row_gates_a(jax.random.fold_in(key_list[7], 71), 0),
        "first_column_gates": draw_first_column_gates(jax.random.fold_in(key_list[7], 71), 0),
        "row_gates_b": draw_row_gates_b(jax.random.fold_in(key_list[7], 71), 0),
        "col_gates_b": draw_col_gates_b(jax.random.fold_in(key_list[7], 71), 0),
        "modes": draw_modes(jax.random.fold_in(key_list[7], 71), 0),
        "outcomes": touch_ends(jax.random.randint(key_list[6], (MEASURED_MODES // 2,), 0, 2), jax.random.fold_in(key_list[6], 1), 0, 1).astype(jnp.int32),
    }


HIGH = lax.Precision.HIGHEST

def rotate_rows(field, gates, offset):
    total = field.shape[0]
    width = gates.shape[1]
    moved = jnp.roll(field, -offset, 0).reshape(total // width, width, -1)
    rotated_slab = jnp.einsum('kab,kbc->kac', gates.astype(jnp.float32), moved, precision=HIGH)
    return jnp.roll(rotated_slab.reshape(total, -1), offset, 0)

def rotate_cols(field, gates, offset):
    total = field.shape[1]
    width = gates.shape[1]
    moved = jnp.roll(field, -offset, 1).reshape(field.shape[0], total // width, width)
    rotated_slab = jnp.einsum('rkb,kab->rka', moved, gates.astype(jnp.float32), precision=HIGH)
    return jnp.roll(rotated_slab.reshape(field.shape[0], total), offset, 1)

def pairing(outcomes):
    signs = jnp.repeat(2.0 * outcomes.astype(jnp.float32) - 1.0, 2)
    first_factor = jnp.arange(MEASURED_MODES)[:, None]
    second_factor = jnp.arange(MEASURED_MODES)[None, :]
    upper = ((second_factor == first_factor + 1) & (first_factor % 2 == 0)).astype(jnp.float32) * signs[:, None]
    lower = ((first_factor == second_factor + 1) & (second_factor % 2 == 0)).astype(jnp.float32) * signs[None, :]
    return upper - lower

def reference(gamma, row_gates_a, first_column_gates, row_gates_b, col_gates_b, modes, outcomes):
    first_factor = rotate_cols(rotate_rows(gamma, row_gates_a, 0), first_column_gates, 0)
    second_factor = rotate_cols(rotate_rows(first_factor, row_gates_b, RB // 2), col_gates_b, CB // 2)
    panel = second_factor[:, modes]
    measured_rows = second_factor[modes, :]
    block = measured_rows[:, modes]
    matrix = 2.0 * pairing(outcomes) + block
    normal = jnp.dot(matrix.T, matrix, precision=HIGH)
    factor = jnp.linalg.cholesky(normal)
    solved = jax.scipy.linalg.cho_solve((factor, True), jnp.dot(matrix.T, measured_rows, precision=HIGH))
    return second_factor + jnp.dot(panel, solved, precision=HIGH)
```

```python
import jax
import jax.numpy as jnp
from jax import lax
from jax.experimental import pallas as pl
from jax.experimental.pallas import tpu as pltpu
from jax.sharding import PartitionSpec as P

HIGH = lax.Precision.HIGHEST
F32, BF16 = jnp.float32, jnp.bfloat16
NN = (((1,), (0,)), ((), ()))
NT = (((1,), (1,)), ((), ()))


def passed_along(value, axis, by):
    length = lax.axis_size(axis)
    return lax.ppermute(value, axis, [(i, (i + by) % length) for i in range(length)])


def split(x):
    hi = x.astype(BF16)
    return hi, (x - hi.astype(F32)).astype(BF16)


def left(gate, x):
    hi, lo = split(x)
    return lax.dot_general(gate, hi, NN, preferred_element_type=F32) + lax.dot_general(
        gate, lo, NN, preferred_element_type=F32
    )


def right(x, gate):
    hi, lo = split(x)
    return lax.dot_general(hi, gate, NT, preferred_element_type=F32) + lax.dot_general(
        lo, gate, NT, preferred_element_type=F32
    )


def first_layer(x_ref, ra_ref, ca_ref, z_ref):
    z_ref[...] = right(left(ra_ref[0], x_ref[...]), ca_ref[0])


def second_columns(z_ref, from_left, from_right, cb_ref, prev_ref, top_ref, bottom_ref):
    rows, cols = z_ref.shape
    bricks, width, _ = cb_ref.shape
    half, middle = width // 2, rows // 2

    def put(at, value):
        top_ref[:, at : at + value.shape[1]] = value[:middle]
        bottom_ref[:, at : at + value.shape[1]] = value[middle:]

    put(0, right(from_left[...], prev_ref[:, :half]) + right(z_ref[:, :half], prev_ref[:, half:]))
    for j in range(bricks - 1):
        at = half + j * width
        put(at, right(z_ref[:, at : at + width], cb_ref[j]))
    last = cb_ref[bricks - 1]
    put(
        cols - half,
        right(z_ref[:, cols - half :], last[:half, :half]) + right(from_right[...], last[:half, half:]),
    )


def second_rows(top_ref, bottom_ref, above_ref, below_ref, rb_ref, prev_ref, picker_ref, s_ref, picked_ref):
    half = top_ref.shape[0]
    upper = left(prev_ref[:, :half], above_ref[...]) + left(prev_ref[:, half:], top_ref[...])
    lower = left(rb_ref[0, :half, :half], bottom_ref[...]) + left(rb_ref[0, :half, half:], below_ref[...])
    s_ref[:half] = upper
    s_ref[half:] = lower
    whole = jnp.concatenate([upper, lower], axis=0).astype(BF16)
    picked_ref[...] = lax.dot_general(picker_ref[...], whole, NN, preferred_element_type=F32).astype(BF16)


def pairing(outcomes, count):
    signs = jnp.repeat(2.0 * outcomes.astype(F32) - 1.0, 2)
    i = jnp.arange(count)[:, None]
    j = jnp.arange(count)[None, :]
    upper = ((j == i + 1) & (i % 2 == 0)).astype(F32) * signs[:, None]
    lower = ((i == j + 1) & (j % 2 == 0)).astype(F32) * signs[None, :]
    return upper - lower


def gathered(value, axis):
    length = lax.axis_size(axis)
    return [value] + [passed_along(value, axis, -d) for d in range(1, length)]


def spread(value, axis):
    length = lax.axis_size(axis)
    value = jnp.where(lax.axis_index(axis) == 0, value, jnp.zeros_like(value))
    plan = []
    step = 1
    while step < length:
        plan.append((step, min(4, length // step)))
        step *= plan[-1][1]
    if length == 64:
        stages = [(1, 2, 3), (16, 32, 48), (4, 8, 12)]
    else:
        stages = [tuple(k * s for k in range(1, n)) for s, n in plan]
    holders = [0]
    for moves in stages:
        arrived = [lax.ppermute(value, axis, [(h, (h + m) % length) for h in holders]) for m in moves]
        for a in arrived:
            value = value + a
        holders = holders + [(h + m) % length for h in holders for m in moves]
    return value


def shards(gamma, row_gates_a, first_column_gates, row_gates_b, col_gates_b, modes, outcomes):
    rows, cols = gamma.shape
    bricks, width, _ = col_gates_b.shape
    half_row, half_col = rows // 2, width // 2
    count = modes.shape[0]
    total_rows = rows * lax.axis_size("row")
    row = lax.axis_index("row")
    share = count // lax.axis_size("row")

    row_gate_before = passed_along(row_gates_b[0, half_row:], "row", 1)
    col_gate_before = passed_along(col_gates_b[bricks - 1, half_col:], "col", 1)

    z = pl.pallas_call(
        first_layer,
        grid=(bricks,),
        in_specs=[
            pl.BlockSpec((rows, width), lambda j: (0, j)),
            pl.BlockSpec((1, rows, rows), lambda j: (0, 0, 0)),
            pl.BlockSpec((1, width, width), lambda j: (j, 0, 0)),
        ],
        out_specs=pl.BlockSpec((rows, width), lambda j: (0, j)),
        out_shape=jax.ShapeDtypeStruct((rows, cols), F32),
    )(gamma, row_gates_a, first_column_gates)
    from_right = passed_along(z[:, :half_col], "col", -1)
    from_left = passed_along(z[:, cols - half_col :], "col", 1)
    half_shape = jax.ShapeDtypeStruct((half_row, cols), F32)
    top, bottom = pl.pallas_call(second_columns, out_shape=(half_shape, half_shape))(
        z, from_left, from_right, col_gates_b, col_gate_before
    )

    below = passed_along(top, "row", -1)
    above = passed_along(bottom, "row", 1)

    chooser = (jnp.arange(total_rows, dtype=jnp.int32)[:, None] == modes[None, :]).astype(F32)
    panel_top = jnp.dot(top[:, :total_rows], chooser, precision=HIGH)
    panel_bottom = jnp.dot(bottom[:, :total_rows], chooser, precision=HIGH)
    panel_below = passed_along(panel_top, "row", -1)
    panel_above = passed_along(panel_bottom, "row", 1)
    before = row_gate_before.astype(F32)
    own = row_gates_b[0, :half_row].astype(F32)
    upper = jnp.dot(before, jnp.concatenate([panel_above, panel_top], axis=0), precision=HIGH)
    lower = jnp.dot(own, jnp.concatenate([panel_bottom, panel_below], axis=0), precision=HIGH)
    panel = jnp.concatenate([upper, lower], axis=0)
    own_modes = lax.dynamic_slice_in_dim(modes, row * share, share)
    row_ids = row * rows + jnp.arange(rows, dtype=jnp.int32)
    picker = own_modes[:, None] == row_ids[None, :]
    block_rows = jnp.dot(picker.astype(F32), panel, precision=HIGH)
    rolled_block = jnp.concatenate(gathered(block_rows, "row"), axis=0)
    pairs = 2.0 * pairing(outcomes, count)
    rolled_pairs = lax.dynamic_slice_in_dim(jnp.concatenate([pairs, pairs], axis=0), row * share, count)
    rolled = rolled_pairs + rolled_block
    normal = jnp.dot(rolled.T, rolled, precision=HIGH)
    factor = jnp.linalg.cholesky(normal)
    weights = jax.scipy.linalg.cho_solve((factor, True), panel.T)
    weights = jnp.dot(rolled, weights, precision=HIGH).astype(BF16)

    weights, above, below = lax.optimization_barrier((weights, above, below))
    weights = spread(weights, "col")
    second, picked = pl.pallas_call(
        second_rows,
        grid=(bricks,),
        in_specs=[pl.BlockSpec((half_row, width), lambda j: (0, j))] * 4
        + [
            pl.BlockSpec((1, rows, rows), lambda j: (0, 0, 0)),
            pl.BlockSpec((half_row, rows), lambda j: (0, 0)),
            pl.BlockSpec((share, rows), lambda j: (0, 0)),
        ],
        out_specs=(
            pl.BlockSpec((rows, width), lambda j: (0, j)),
            pl.BlockSpec((share, width), lambda j: (0, j)),
        ),
        out_shape=(
            jax.ShapeDtypeStruct((rows, cols), F32),
            jax.ShapeDtypeStruct((share, cols), BF16),
        ),
        cost_estimate=pl.CostEstimate(flops=600_000_000, bytes_accessed=5_000_000, transcendentals=0),
    )(top, bottom, above, below, row_gates_b, row_gate_before, picker.astype(BF16))
    measured = jnp.concatenate(gathered(picked, "row"), axis=0)
    return second + lax.dot_general(
        weights, measured, (((0,), (0,)), ((), ())), preferred_element_type=F32
    )


def solution(mesh):
    in_specs = (
        P("row", "col"),
        P("row", None, None),
        P("col", None, None),
        P("row", None, None),
        P("col", None, None),
        P(),
        P(),
    )
    return jax.shard_map(shards, mesh=mesh, in_specs=in_specs, out_specs=P("row", "col"), check_vma=False)
```
